32 devices in a mesh: dp: 4 (over y, core), expert: 8 (over z, x).
Axes of the slice: x: 2, y: 2, z: 4, core: 2. Of those that a mesh axis runs over, the one named last changes fastest.
Arguments:
- text: bfloat16 [4096, 5120], P(('dp', 'expert')), may hold values from -6 to 6
- patches: bfloat16 [4, 24, 24, 1408], P('dp', None, None, 'expert'), may hold values from -6 to 6
- vis_start: int32 [4], P('dp'), may hold values from 0 to 880
- fc1: bfloat16 [4, 1408, 4096], P(None, 'expert', 'dp'), may hold values from -0.078125 to 0.078125
- fc2: bfloat16 [4096, 4096], P('expert', 'dp'), may hold values from -0.09375 to 0.09375
- proj: bfloat16 [4096, 5120], P('expert', 'dp'), may hold values from -0.09375 to 0.09375
- norm_gain: bfloat16 [5120], replicated, may hold values from 0.099609375 to 1.8984375
- router: bfloat16 [5120, 8], replicated, may hold values from -0.078125 to 0.078125
- routes: int32 [4096, 1], P(('dp', 'expert')), may hold values from 0 to 7; in each aligned block of 128 rows (0 to 127, 128 to 255, ...) at most 20 rows name the same one
- gate_w: bfloat16 [8, 5120, 4096], P('expert', None, 'dp'), may hold values from -0.15625 to 0.15625
- up_w: bfloat16 [8, 5120, 4096], P('expert', None, 'dp'), may hold values from -0.15625 to 0.15625
- down_w: bfloat16 [8, 4096, 5120], P('expert', 'dp'), may hold values from -0.09375 to 0.09375
Outputs:
- layer_out: bfloat16 [4096, 5120], P(('dp', 'expert'))
The draws below stay inside these ranges and needn't reach their ends.
Inputs may be any that keep to these rules, and one draw needn't show every extreme that they name: `routes`: among the 128 positions of one device each expert is named at most 20 times. The image of sequence n fills the 144 positions from vis_start[n] on.
All inputs are finite; a program needn't handle non-finite values.
Results may differ from the reference program's by a relative error of at most 0.024.
Values may be sent and summed in bfloat16 or wider, within the bound.
A program may use at most 128 MiB of HBM per device.

```python
import math
import jax
import jax.numpy as jnp
import numpy as np
from jax import lax

D = 5120
FF = 4096
VC = 1408
VA = 4096
GRID = 24
TOK_DEV = 128
VT = 144
EXPERTS = 8
CAP = 20
SEQ = 1024
IMAGES = 4
TOKENS = 4096
N_DP = 4
DEVICES = 32


def plant(result, stream_key, low, largest):
    longest = result.shape.index(max(result.shape))
    spots = []
    for shift in (0, 1):
        where = [jax.random.randint(jax.random.fold_in(stream_key, axis), (), 0, length) for axis, length in enumerate(result.shape)]
        where[longest] = (where[longest] + shift) % result.shape[longest]
        spots.append(tuple(where))
    return result.at[spots[0]].set(low).at[spots[1]].set(largest)


def shard_levels(stream_key, extent, split, smallest, top_value):
    gain = 1.0
    for position, parts in split:
        heights = jax.random.uniform(jax.random.fold_in(jax.random.fold_in(stream_key, 6), position), (parts,), jnp.float32, smallest / len(split), top_value / len(split))
        gain = gain * jnp.repeat(jnp.exp(heights), extent[position] // parts).reshape((-1,) + (1,) * (len(extent) - 1 - position))
    return gain


def deal_out(key, own, number, rows, amount, top, bound, slope):
    ranking = jax.random.permutation(key, amount)
    heavy_load, common = load_shares(amount, rows * top, bound, slope, True), load_shares(amount, rows * top, bound, slope, False)
    places = jnp.arange(amount)

    def named(tallies, rotation):
        used = int((tallies > 0).sum())
        fixed = max(1, used // 4)
        passed = fixed + (places - fixed + rotation * (used - fixed)) % max(1, amount - fixed)
        return jnp.zeros((amount,), jnp.int32).at[ranking[jnp.where(places < fixed, places, passed)]].set(jnp.asarray(tallies, jnp.int32))

    tallies = jnp.where(number % 4 == 0, named(heavy_load, number // 4), named(common, number - number // 4 - 1))
    mixed = jax.random.permutation(jax.random.fold_in(own, 3), amount)
    source_of, taker = mixed[0:amount // 2 * 2:2], mixed[1:amount // 2 * 2:2]
    slack = jnp.minimum(tallies[source_of] - 1, bound - tallies[taker]) // 2
    slack = jnp.where((source_of == ranking[0]) | (taker == ranking[0]) | (tallies[taker] == 0), 0, jnp.maximum(slack, 0))
    passed = jax.random.randint(jax.random.fold_in(own, 4), (amount // 2,), 0, 1 << 20) % (slack + 1)
    tallies = tallies.at[source_of].add(-passed).at[taker].add(passed)
    items = jnp.searchsorted(jnp.cumsum(tallies), jnp.arange(rows * top), side="right").astype(jnp.int32)
    listing = items.reshape(top, rows).T
    listing = listing[jax.random.permutation(jax.random.fold_in(own, 1), rows)]
    rotation = jax.random.randint(jax.random.fold_in(own, 2), (rows, 1), 0, top)
    return jnp.take_along_axis(listing, (jnp.arange(top)[None, :] + rotation) % top, axis=1)


def load_shares(count, total, bound, lean, full):
    portions = [(1 << 20) // math.isqrt(rank ** lean) + 1 for rank in range(1, count + 1)]
    largest = bound if full else min(bound, max(-(-total // count), total * portions[0] // sum(portions)))
    least = 1 if total - largest >= count - 1 else 0
    counts, rest = [largest] + [least] * (count - 1), total - largest - least * (count - 1)
    while rest > 0:
        candidates = [i for i in range(1, count) if counts[i] < largest] or [i for i in range(1, count) if counts[i] < bound]
        whole, left = sum([portions[i] for i in candidates]), rest
        for i in candidates:
            extra = min(bound - counts[i], max(1, left * portions[i] // whole), rest)
            counts[i] = counts[i] + extra
            rest = rest - extra
    return np.array(counts)


def bell_draw(rng, shape, spread, reach, split=(), held_as=jnp.bfloat16):
    array = jax.random.normal(rng, shape, jnp.float32) * spread
    if len(split) > 0:
        array = shard_levels(rng, shape, split, -0.22, 0.18) * array
    return jnp.clip(array, min=-reach, max=reach).astype(held_as)


def setup_inputs(seed: int = 0) -> dict:
    splits = jax.random.split(jax.random.key(seed), 13)
    text = bell_draw(splits[0], (TOKENS, D), 1.0, 6.0, ((0, 32),))
    patches = bell_draw(splits[1], (IMAGES, GRID, GRID, VC), 1.0, 6.0, ((0, 4), (3, 8)))
    vis_start = plant(jax.random.randint(splits[2], (IMAGES,), 0, SEQ - VT + 1), jax.random.fold_in(splits[2], 1), 0, SEQ - VT).astype(jnp.int32)
    fc1 = bell_draw(splits[3], (4, VC, VA), (4 * VC) ** -0.5, 0.078125, ((1, 8), (2, 4)))
    fc2 = bell_draw(splits[4], (VA, VA), VA ** -0.5, 0.09375, ((0, 8), (1, 4)))
    proj = bell_draw(splits[5], (VA, D), VA ** -0.5, 0.09375, ((0, 8), (1, 4)))
    norm_gain = jnp.clip(1.0 + 0.18 * jax.random.normal(splits[6], (D,), jnp.float32), 0.099609375, 1.8984375).astype(jnp.bfloat16)
    router = bell_draw(splits[7], (D, EXPERTS), D ** -0.5, 0.078125)
    routes_keys = jax.random.split(jax.random.fold_in(splits[8], 1), TOKENS // TOK_DEV)
    routes_turns = jax.random.permutation(jax.random.fold_in(splits[8], 3), TOKENS // TOK_DEV)
    routes = jax.vmap(lambda own, number: deal_out(jax.random.fold_in(splits[8], 2), own, number, TOK_DEV, EXPERTS, 1, CAP, 1))(routes_keys, routes_turns).reshape((TOKENS, 1))
    gate_w = bell_draw(splits[9], (EXPERTS, D, FF), (D // 4) ** -0.5, 0.15625, ((0, 8), (2, 4)))
    up_w = bell_draw(splits[10], (EXPERTS, D, FF), (D // 4) ** -0.5, 0.15625, ((0, 8), (2, 4)))
    down_w = bell_draw(splits[11], (EXPERTS, FF, D), FF ** -0.5, 0.09375, ((0, 8), (1, 4)))
    return {"text": text, "patches": patches, "vis_start": vis_start, "fc1": fc1, "fc2": fc2, "proj": proj, "norm_gain": norm_gain, "router": router, "routes": routes, "gate_w": gate_w, "up_w": up_w, "down_w": down_w}


EPSILON = 1e-05

def expert_run(operands):
    token_rows, gate_mat, up_mat, down_mat = operands
    gate_act = jnp.dot(token_rows, gate_mat, preferred_element_type=jnp.float32)
    up_act = jnp.dot(token_rows, up_mat, preferred_element_type=jnp.float32)
    hidden = (jax.nn.silu(gate_act) * up_act).astype(jnp.bfloat16)
    slice_width = FF // N_DP
    partials = jnp.einsum('snf,nfd->nsd', hidden.reshape(-1, N_DP, slice_width).astype(jnp.float32), down_mat.reshape(N_DP, slice_width, D).astype(jnp.float32))
    rounded = lax.optimization_barrier(partials.astype(jnp.bfloat16))
    return rounded.astype(jnp.float32).sum(axis=0).astype(jnp.bfloat16)

def pick_rows(visual_rows, index_rows):
    return jnp.take(visual_rows, index_rows, axis=0)

def reference(text, patches, vis_start, fc1, fc2, proj, norm_gain, router, routes, gate_w, up_w, down_w):
    half_grid = GRID // 2
    shuffled = patches.reshape(IMAGES, half_grid, 2, half_grid, 2, VC)
    shuffled = shuffled.transpose(0, 1, 3, 2, 4, 5).reshape(IMAGES * VT, 4 * VC)
    pre_act = jnp.dot(shuffled, fc1.reshape(4 * VC, VA), preferred_element_type=jnp.float32)
    activated = jax.nn.gelu(pre_act, approximate=False).astype(jnp.bfloat16)
    middle_pre = jnp.dot(activated, fc2, preferred_element_type=jnp.float32)
    middle = jax.nn.gelu(middle_pre, approximate=False).astype(jnp.bfloat16)
    visual = jnp.dot(middle, proj, preferred_element_type=jnp.float32).astype(jnp.bfloat16)
    visual = visual.reshape(IMAGES, VT, D)
    sequences = text.reshape(IMAGES, SEQ, D)
    positions = jnp.arange(SEQ, dtype=jnp.int32)
    offsets = positions[None, :] - vis_start[:, None]
    in_image = (offsets >= 0) & (offsets < VT)
    picked = jax.vmap(pick_rows)(visual, jnp.clip(offsets, 0, VT - 1).astype(jnp.int32))
    embedded = jnp.where(in_image[:, :, None], picked, sequences).reshape(TOKENS, D)
    embed_f32 = embedded.astype(jnp.float32)
    mean_square = lax.optimization_barrier(jnp.mean(embed_f32 * embed_f32, axis=-1, keepdims=True))
    normed = (embed_f32 * lax.rsqrt(mean_square + EPSILON) * norm_gain.astype(jnp.float32)).astype(jnp.bfloat16)
    logits = jnp.dot(normed, router, preferred_element_type=jnp.float32)
    expert_id = routes[:, 0]
    one_hot = expert_id[:, None] == jnp.arange(EXPERTS, dtype=jnp.int32)[None, :]
    gate_score = jax.nn.sigmoid(lax.optimization_barrier(jnp.sum(jnp.where(one_hot, logits, 0.0), axis=-1)))
    routed_in = (normed.astype(jnp.float32) * gate_score[:, None]).astype(jnp.bfloat16)
    blocks = one_hot.astype(jnp.int32).reshape(DEVICES, TOK_DEV, EXPERTS)
    earlier = (jnp.cumsum(blocks, axis=1) - blocks).reshape(TOKENS, EXPERTS)
    slot_rank = lax.optimization_barrier(jnp.sum(jnp.where(one_hot, earlier, 0), axis=-1)).astype(jnp.int32)
    slot = jnp.arange(TOKENS, dtype=jnp.int32) // TOK_DEV * CAP + slot_rank
    buffer = jnp.zeros((EXPERTS, DEVICES * CAP, D), jnp.bfloat16).at[expert_id, slot].set(routed_in)
    outputs = lax.map(expert_run, (buffer, gate_w, up_w, down_w))
    expert_out = outputs[expert_id, slot]
    return (embed_f32 + expert_out.astype(jnp.float32)).astype(jnp.bfloat16)
```

```python
import functools

import jax
import jax.numpy as jnp
from jax import lax
from jax.experimental import pallas as pl
from jax.experimental.pallas import tpu as pltpu
from jax.sharding import PartitionSpec as P

EPSILON = 1e-05
MESH = pl.DeviceIdType.MESH


def send(src, dst, send_sem, recv_sem, d, e):
    return pltpu.make_async_remote_copy(
        src_ref=src,
        dst_ref=dst,
        send_sem=send_sem,
        recv_sem=recv_sem,
        device_id={"dp": d, "expert": e},
        device_id_type=MESH,
    )


def greet(d, e):
    pl.semaphore_signal(
        pltpu.get_barrier_semaphore(),
        inc=1,
        device_id={"dp": d, "expert": e},
        device_id_type=MESH,
    )


def turn(index, step):
    bit = 1
    while bit <= step:
        if step & bit:
            index = index + bit - 2 * bit * lax.rem(index // bit, 2)
        bit *= 2
    return index


def far_first(count):
    order, high = [], count // 2
    while high:
        order += range(high, 2 * high)
        high //= 2
    return order + [0]


def mixed(count):
    near, far = list(range(count // 2)), list(range(count // 2, count))
    order = near[:2]
    for i, step in enumerate(far):
        order.append(step)
        if i > 0 and i + 1 < len(near):
            order.append(near[i + 1])
    return order


def keep(src, dst, bounce, sem):
    first = pltpu.make_async_copy(src, bounce, sem)
    first.start()
    first.wait()
    second = pltpu.make_async_copy(bounce, dst, sem)
    second.start()
    second.wait()


def call(kernel, x, out_shape, scratch, sem_counts, collective_id, space=pl.ANY):
    return pl.pallas_call(
        kernel,
        out_shape=jax.ShapeDtypeStruct(out_shape, x.dtype),
        in_specs=[pl.BlockSpec(memory_space=space)],
        out_specs=pl.BlockSpec(memory_space=space),
        scratch_shapes=[pltpu.VMEM(shape, x.dtype) for shape in scratch]
        + [pltpu.SemaphoreType.DMA]
        + [pltpu.SemaphoreType.DMA((count,)) for count in sem_counts],
        compiler_params=pltpu.CompilerParams(
            collective_id=collective_id, has_side_effects=True
        ),
    )(x)


def cross_kernel(n_dp, x, out, landed, paired, summed, loc, s1, r1, s2, r2, s3, r3):
    d, e = lax.axis_index("dp"), lax.axis_index("expert")
    side, place = lax.rem(e, 2), e // 2
    width = out.shape[2]
    mine = pl.ds(pl.multiple_of(side * width, 128), width)
    theirs = pl.ds(pl.multiple_of((1 - side) * width, 128), width)
    mate = place * 2 + 1 - side
    for j in range(1, n_dp):
        greet(lax.rem(d + j, n_dp), e)
        greet(d, lax.rem(place + j, n_dp) * 2 + side)
    greet(d, mate)
    pl.semaphore_wait(pltpu.get_barrier_semaphore(), 2 * n_dp - 1)
    first, second = [], []
    for j in range(1, n_dp):
        to_d = lax.rem(d + j, n_dp)
        first.append(send(x.at[to_d], landed.at[j], s1.at[j], r1.at[j], to_d, e))
        first[-1].start()

    def source(j):
        return x.at[d] if j == 0 else landed.at[j]

    def third(j):
        owner = lax.rem(d + n_dp - j, n_dp)
        moved = send(
            summed.at[j], out.at[place], s3.at[j], r3.at[place], d, owner * 2 + side
        )
        return owner != place, moved

    def add(j):
        second[j].wait_recv()
        own = x[d, :, mine] if j == 0 else landed[j, :, mine]
        total = own.astype(jnp.float32) + paired[j].astype(jnp.float32)
        summed[j] = total.astype(summed.dtype)
        away, _ = third(j)

        @pl.when(jnp.logical_not(away))
        def _():
            out[place] = total.astype(out.dtype)

    for j in range(n_dp):
        if j > 0:
            first[j - 1].wait_recv()
        second.append(send(source(j).at[:, theirs], paired.at[j], s2.at[j], r2.at[j], d, mate))
        second[j].start()
        if j > 0:
            add(j - 1)
        if j > 1:
            away, moved = third(j - 2)
            pl.when(away)(moved.start)
    add(n_dp - 1)
    for j in (n_dp - 2, n_dp - 1):
        away, moved = third(j)
        pl.when(away)(moved.start)
    for other in range(n_dp):
        @pl.when(other != place)
        def _():
            send(
                summed.at[0], out.at[other], s3.at[0], r3.at[other], d, other * 2 + side
            ).wait_recv()
    for j in range(n_dp):
        away, moved = third(j)
        pl.when(away)(moved.wait_send)
    for moved in first + second:
        moved.wait_send()


def cross(part, n_dp, collective_id):
    x = part.astype(jnp.bfloat16).reshape(n_dp, part.shape[0] // n_dp, part.shape[1])
    width = x.shape[2] // 2
    spare = -width % 128
    if spare:
        x = x.reshape(n_dp, x.shape[1], 2, width)
        x = jnp.pad(x, ((0, 0), (0, 0), (0, 0), (0, spare)))
        x = x.reshape(n_dp, x.shape[1], 2 * (width + spare))
    half = (n_dp, x.shape[1], width + spare)
    out = call(
        functools.partial(cross_kernel, n_dp),
        x, half, (x.shape, half, half), (n_dp,) * 6, collective_id, pltpu.VMEM,
    )
    return out[:, :, :width] if spare else out


def gather_expert_kernel(n_exp, x, out, bounce, loc, s_sem, r_sem, sp_sem, rp_sem):
    d, e = lax.axis_index("dp"), lax.axis_index("expert")
    side, place = lax.rem(e, 2), e // 2
    half = n_exp // 2
    mate = place * 2 + 1 - side
    greet(d, mate)
    for i in range(1, half):
        greet(d, lax.rem(place + i, half) * 2 + side)
    pl.semaphore_wait(pltpu.get_barrier_semaphore(), half)
    near = [send(x, out.at[e], sp_sem.at[0], rp_sem.at[0], d, mate)]
    near[0].start()
    far = []
    for i in range(1, half):
        to_e = lax.rem(place + i, half) * 2 + side
        far.append(send(x, out.at[e], s_sem.at[i], r_sem.at[i], d, to_e))
        far[-1].start()
    keep(x, out.at[e], bounce, loc)
    for i in range(1, half):
        far[i - 1].wait_recv()
        block = out.at[lax.rem(place + half - i, half) * 2 + side]
        near.append(send(block, block, sp_sem.at[i], rp_sem.at[i], d, mate))
        near[i].start()
    for moved in near:
        moved.wait()
    for moved in far:
        moved.wait_send()


def gather_expert(x, n_exp, collective_id):
    return call(
        functools.partial(gather_expert_kernel, n_exp),
        x, (n_exp,) + x.shape, (x.shape,), (n_exp // 2,) * 4, collective_id, pltpu.VMEM,
    )


def gather_dp_kernel(n_dp, x, out, bounce, loc, s_sem, r_sem, sp_sem, rp_sem):
    d, e = lax.axis_index("dp"), lax.axis_index("expert")
    ny = n_dp // 2
    y, c = d // 2, lax.rem(d, 2)
    partner = y * 2 + 1 - c
    greet(partner, e)
    for i in range(1, ny):
        greet(lax.rem(y + i, ny) * 2 + c, e)
    pl.semaphore_wait(pltpu.get_barrier_semaphore(), ny)
    far = [
        send(x, out.at[d], s_sem.at[i], r_sem.at[i], lax.rem(y + i, ny) * 2 + c, e)
        for i in range(1, ny)
    ]
    for moved in far:
        moved.start()
    near = [send(x, out.at[d], sp_sem.at[0], rp_sem.at[0], partner, e)]
    near[0].start()
    keep(x, out.at[d], bounce, loc)
    for i in range(1, ny):
        far[i - 1].wait_recv()
        slot = lax.rem(y + ny - i, ny) * 2 + c
        near.append(send(out.at[slot], out.at[slot], sp_sem.at[i], rp_sem.at[i], partner, e))
        near[i].start()
    for moved in near:
        moved.wait()
    for moved in far:
        moved.wait_send()


def gather_dp(x, n_dp, collective_id):
    ny = n_dp // 2
    return call(
        functools.partial(gather_dp_kernel, n_dp),
        x, (n_dp,) + x.shape, (x.shape,), (ny, ny, ny, ny), collective_id, pltpu.VMEM,
    )


def dispatch_kernel(n_dp, n_exp, x, out, bounce, loc, s1, r1, sy, ry, sp, rp):
    d, e = lax.axis_index("dp"), lax.axis_index("expert")
    ny = n_dp // 2
    y, c = d // 2, lax.rem(d, 2)
    partner = y * 2 + 1 - c
    greet(partner, e)
    for i in range(1, n_exp):
        greet(d, turn(e, i))
    for j in range(1, ny):
        greet(lax.rem(y + j, ny) * 2 + c, e)
    pl.semaphore_wait(pltpu.get_barrier_semaphore(), n_exp + ny - 1)
    first, far, near = {}, {}, []
    for i in far_first(n_exp):
        if i > 0:
            to_e = turn(e, i)
            first[i] = send(x.at[to_e], out.at[d, e], s1.at[i], r1.at[i], d, to_e)
            first[i].start()

    def spread(i):
        slot = turn(e, i)
        if i > 0:
            first[i].wait_recv()
        block = x.at[e] if i == 0 else out.at[d, slot]
        for j in range(1, ny):
            index = i * ny + j
            moved = send(
                block, out.at[d, slot], sy.at[index], ry.at[index], lax.rem(y + j, ny) * 2 + c, e
            )
            moved.start()
            far[index] = moved
        moved = send(block, out.at[d, slot], sp.at[i * ny], rp.at[i * ny], partner, e)
        moved.start()
        near.append(moved)

    def relay(i):
        slot = turn(e, i)
        for j in range(1, ny):
            index = i * ny + j
            far[index].wait_recv()
            block = out.at[lax.rem(y + ny - j, ny) * 2 + c, slot]
            moved = send(block, block, sp.at[index], rp.at[index], partner, e)
            moved.start()
            near.append(moved)

    order = mixed(n_exp)
    for at, i in enumerate(order):
        spread(i)
        if i == 0:
            keep(x.at[e], out.at[d, e], bounce, loc)
        if at > 1:
            relay(order[at - 2])
    relay(order[-2])
    relay(order[-1])
    for moved in near:
        moved.wait()
    for moved in list(first.values()) + list(far.values()):
        moved.wait_send()


def dispatch(x, n_dp, n_exp, collective_id):
    count = n_dp // 2 * n_exp
    return call(
        functools.partial(dispatch_kernel, n_dp, n_exp),
        x, (n_dp,) + x.shape, (x.shape[1:],), (n_exp, n_exp) + (count,) * 4, collective_id,
    )


def swap_kernel(n_dp, x, out, bounce, loc, s_sem, r_sem):
    d, e = lax.axis_index("dp"), lax.axis_index("expert")
    ny = n_dp // 2
    y, c = d // 2, lax.rem(d, 2)
    partner = y * 2 + 1 - c
    greet(partner, e)
    pl.semaphore_wait(pltpu.get_barrier_semaphore(), 1)
    copies = [
        send(x.at[i, 1 - c], out.at[i], s_sem.at[i], r_sem.at[i], partner, e)
        for i in range(ny)
    ]
    for moved in copies:
        moved.start()
    for moved in copies:
        moved.wait()


def swap(x, n_dp, collective_id):
    ny = n_dp // 2
    return call(
        functools.partial(swap_kernel, n_dp),
        x, (ny,) + x.shape[2:], ((16, 128),), (ny, ny), collective_id,
    )


def home_kernel(n_dp, n_exp, x, out, landed, summed, loc, s1, r1, s2, r2):
    d, e = lax.axis_index("dp"), lax.axis_index("expert")
    ny = n_dp // 2
    y, c = d // 2, lax.rem(d, 2)
    for i in range(1, n_exp):
        greet(d, turn(e, i))
    for j in range(1, ny):
        greet(lax.rem(y + j, ny) * 2 + c, e)
    pl.semaphore_wait(pltpu.get_barrier_semaphore(), n_exp + ny - 2)
    columns = [turn(e, i) for i in far_first(n_exp)]
    first, second = [], []
    for i, column in enumerate(columns):
        for j in range(1, ny):
            to_y, index = lax.rem(y + j, ny), i * ny + j
            first.append(
                send(
                    x.at[to_y, column], landed.at[j, i],
                    s1.at[index], r1.at[index], to_y * 2 + c, e,
                )
            )
            first[-1].start()
    for i, column in enumerate(columns):
        total = x[y, column].astype(jnp.float32)
        for j in range(1, ny):
            first[i * (ny - 1) + j - 1].wait_recv()
            total = total + landed[j, i].astype(jnp.float32)
        if i < n_exp - 1:
            summed[i] = total.astype(summed.dtype)
            second.append(send(summed.at[i], out.at[e], s2.at[i], r2.at[i], d, column))
        else:
            out[e] = total.astype(out.dtype)
        if i > 0:
            second[i - 1].start()
    for moved in second:
        moved.wait()
    for moved in first:
        moved.wait_send()


def send_home(x, n_dp, n_exp, collective_id):
    ny = n_dp // 2
    return call(
        functools.partial(home_kernel, n_dp, n_exp),
        x, x.shape[1:], (x.shape, x.shape[1:]),
        (ny * n_exp, ny * n_exp, n_exp, n_exp), collective_id, pltpu.VMEM,
    )


def add_blocks(blocks):
    return jnp.sum(blocks.astype(jnp.float32), axis=0)


def on_device(
    text, patches, vis_start, fc1, fc2, proj, norm_gain, router, routes, gate_w, up_w, down_w
):
    expert_count = lax.axis_size("expert")
    my_column = lax.axis_index("expert")
    row_count = text.shape[0]
    feature = text.shape[1]
    grid_size = patches.shape[1]
    half_grid = grid_size // 2
    local_channels = patches.shape[3]
    vis_count = half_grid * half_grid
    shuffled = patches.reshape(half_grid, 2, half_grid, 2, local_channels)
    shuffled = shuffled.transpose(0, 2, 1, 3, 4).reshape(vis_count, 4 * local_channels)
    n_dp = lax.axis_size("dp")
    shuffled = gather_dp(shuffled, n_dp, 0).reshape(n_dp * vis_count, 4 * local_channels)
    weights = fc1.reshape(4 * local_channels, fc1.shape[2])
    pre_part = jnp.dot(shuffled, weights, preferred_element_type=jnp.float32)
    pre_act = add_blocks(cross(pre_part, n_dp, 1))
    activated = jax.nn.gelu(pre_act, approximate=False).astype(jnp.bfloat16)
    activated = gather_dp(activated, n_dp, 2).reshape(n_dp * vis_count, fc2.shape[0])
    middle_part = jnp.dot(activated, fc2, preferred_element_type=jnp.float32)
    middle_pre = add_blocks(cross(middle_part, n_dp, 3))
    middle = jax.nn.gelu(middle_pre, approximate=False).astype(jnp.bfloat16)
    middle = gather_dp(middle, n_dp, 4).reshape(n_dp * vis_count, proj.shape[0])
    visual_part = jnp.dot(middle, proj, preferred_element_type=jnp.float32)
    visual_own = add_blocks(
        cross(visual_part, n_dp, 5)
    ).astype(jnp.bfloat16)
    visual = gather_expert(visual_own, expert_count, 6)
    visual = visual.transpose(1, 0, 2).reshape(vis_count, feature)
    positions = my_column * row_count + jnp.arange(row_count, dtype=jnp.int32)
    offsets = positions - vis_start[0]
    in_image = (offsets >= 0) & (offsets < vis_count)
    picked = jnp.take(visual, jnp.clip(offsets, 0, vis_count - 1), axis=0)
    embedded = jnp.where(in_image[:, None], picked, text)
    embed_f32 = embedded.astype(jnp.float32)
    mean_square = jnp.mean(embed_f32 * embed_f32, axis=-1, keepdims=True)
    normed = (embed_f32 * lax.rsqrt(mean_square + EPSILON) * norm_gain.astype(jnp.float32)).astype(
        jnp.bfloat16
    )
    logits = jnp.dot(normed, router, preferred_element_type=jnp.float32)
    experts_all = router.shape[1]
    expert_id = routes[:, 0]
    one_hot = expert_id[:, None] == jnp.arange(experts_all, dtype=jnp.int32)[None, :]
    gate_score = jax.nn.sigmoid(jnp.sum(jnp.where(one_hot, logits, 0.0), axis=-1))
    routed_in = (normed.astype(jnp.float32) * gate_score[:, None]).astype(jnp.bfloat16)
    capacity = max(2, row_count * 5 // (4 * expert_count))
    capacity += -capacity % 8
    row_ids = jnp.arange(row_count, dtype=jnp.int32)
    earlier_mask = (row_ids[None, :] < row_ids[:, None]).astype(jnp.bfloat16)
    earlier_counts = jnp.dot(
        earlier_mask, one_hot.astype(jnp.bfloat16), preferred_element_type=jnp.float32
    )
    slot_rank = jnp.sum(jnp.where(one_hot, earlier_counts, 0.0), axis=-1).astype(jnp.int32)
    slot_key = expert_id * capacity + slot_rank
    slot_ids = jnp.arange(experts_all * capacity, dtype=jnp.int32)
    dispatch_table = (slot_ids[:, None] == slot_key[None, :]).astype(jnp.bfloat16)
    outgoing = jnp.dot(dispatch_table, routed_in, preferred_element_type=jnp.float32).astype(
        jnp.bfloat16
    )
    outgoing = outgoing.reshape(experts_all, capacity, feature)
    gathered = dispatch(outgoing, n_dp, expert_count, 7)
    flat_rows = gathered.reshape(-1, feature)
    gate_act = jnp.dot(flat_rows, gate_w[0], preferred_element_type=jnp.float32)
    up_act = jnp.dot(flat_rows, up_w[0], preferred_element_type=jnp.float32)
    hidden = (jax.nn.silu(gate_act) * up_act).astype(jnp.bfloat16)
    partial_value = jnp.dot(hidden, down_w[0], preferred_element_type=jnp.float32)
    slots = experts_all * capacity
    partial_value = partial_value.astype(jnp.bfloat16).reshape(n_dp // 2, 2, slots, feature)
    core = lax.rem(lax.axis_index("dp"), 2)
    mine = lax.dynamic_index_in_dim(partial_value, core, axis=1, keepdims=False)
    pair = mine.astype(jnp.float32) + swap(partial_value, n_dp, 8).astype(jnp.float32)
    pair = pair.astype(jnp.bfloat16).reshape(n_dp // 2, experts_all, capacity, feature)
    expert_out = send_home(pair, n_dp, expert_count, 9)
    combined = lax.dot_general(
        dispatch_table,
        expert_out.reshape(experts_all * capacity, feature),
        (((0,), (0,)), ((), ())),
        preferred_element_type=jnp.float32,
    )
    return (embed_f32 + combined).astype(jnp.bfloat16)


def solution(mesh):
    return jax.shard_map(
        on_device,
        mesh=mesh,
        in_specs=(
            P(("dp", "expert"), None),
            P("dp", None, None, "expert"),
            P("dp"),
            P(None, "expert", "dp"),
            P("expert", "dp"),
            P("expert", "dp"),
            P(),
            P(),
            P(("dp", "expert"), None),
            P("expert", None, "dp"),
            P("expert", None, "dp"),
            P("expert", "dp", None),
        ),
        out_specs=P(("dp", "expert"), None),
        check_vma=False,
    )
```
